32 devices in a mesh: outer: 4 (over y, x), inner: 8 (over z, core).
Axes of the slice: x: 2, y: 2, z: 4, core: 2. Of those that a mesh axis runs over, the one named last changes fastest.
Arguments:
- queries: bfloat16 [4096, 2048], P(('outer', 'inner')), may hold values from -6 to 6
- key_rows: bfloat16 [4096, 2048], P(('outer', 'inner')), may hold values from -6 to 6
- value_rows: bfloat16 [4096, 2048], P(('outer', 'inner')), may hold values from -6 to 6
- beta_logit: bfloat16 [4096, 16], P(('outer', 'inner')), may hold values from -8 to 2, as said below
- log_gate: bfloat16 [4096, 16], P(('outer', 'inner')), may hold values from -1 to 0, as said below
- out_grad: bfloat16 [4096, 2048], P(('outer', 'inner')), may hold values from -6 to 6
- block_states: float32 [4, 16, 128, 128], P('outer', 'inner'), may hold values from -4 to 4
Outputs:
- query_gradient: bfloat16 [4096, 2048], P(('outer', 'inner'))
- grad_keys: bfloat16 [4096, 2048], P(('outer', 'inner'))
- grad_values: bfloat16 [4096, 2048], P(('outer', 'inner'))
- grad_beta: bfloat16 [4096, 16], P(('outer', 'inner'))
- grad_gate: bfloat16 [4096, 16], P(('outer', 'inner'))
The draws below stay inside these ranges and needn't reach their ends.
Inputs may be any that keep to these rules, and one draw needn't show every extreme that they name: `beta_logit`: within each head the logits lie within 1 of a level drawn for each head. `log_gate`: negative in every entry.
All inputs are finite; a program needn't handle non-finite values.
Results may differ from the reference program's by a relative error of at most 0.002.
Values may be sent and summed in bfloat16 or wider, within the bound.
A program may use at most 128 MiB of HBM per device.

```python
import math
import jax
import jax.numpy as jnp
from jax import lax

H = 16
DK = 128
DV = 128
GROUP = 128
TOK_DEV = 128
TOKENS = 4096
N_OUTER = 4


def quick_heads(key):
    fast_share = 0.5
    return jax.random.bernoulli(jax.random.fold_in(key, 11), fast_share, (H,))


def draw_key_rows(key, part):
    sub_key = jax.random.fold_in(key, 53)
    shared = jax.random.normal(jax.random.fold_in(sub_key, 1), (H, DK), jnp.float32)
    amplitude = jax.random.uniform(jax.random.fold_in(sub_key, 2), (H,), jnp.float32, 0.8, 1.2)
    noise = jax.random.normal(jax.random.fold_in(sub_key, 3), (TOKENS, H, DK), jnp.float32)
    rows = noise + amplitude[None, :, None] * shared[None, :, :]
    return jnp.clip(rows, -6.0, 6.0).reshape(TOKENS, H * DK).astype(jnp.bfloat16)


def draw_beta_logit(key, part):
    sub_key = jax.random.fold_in(key, 23)
    centers = jax.random.uniform(jax.random.fold_in(sub_key, 1), (H,), jnp.float32, -6.5, -1.5)
    spread = jax.random.uniform(jax.random.fold_in(sub_key, 2), (TOKENS, H), jnp.float32, -1.0, 1.0)
    return (centers[None, :] + spread).astype(jnp.bfloat16)


def draw_log_gate(key, part):
    quick = quick_heads(key)
    sub_key = jax.random.fold_in(key, 37)
    quick_rate = jnp.exp(jax.random.uniform(jax.random.fold_in(sub_key, 1), (H,), jnp.float32, math.log(1.0 / 50.0), math.log(1.0 / 30.0)))
    slow_rate = jnp.exp(jax.random.uniform(jax.random.fold_in(sub_key, 2), (H,), jnp.float32, math.log(0.05), math.log(0.15))) / TOKENS
    decay_rate = jnp.where(quick, quick_rate, slow_rate)
    device_count = TOKENS // TOK_DEV
    device_factor = jnp.exp(jax.random.uniform(jax.random.fold_in(sub_key, 3), (device_count, H), jnp.float32, math.log(0.5), math.log(2.0)))
    owner = jnp.arange(TOKENS) // TOK_DEV
    per_token = device_factor[owner]
    rough = jax.random.uniform(jax.random.fold_in(sub_key, 4), (TOKENS, H), jnp.float32, 0.5, 1.5)
    initial_gate = -decay_rate[None, :] * per_token * rough
    spots = jax.random.randint(jax.random.fold_in(sub_key, 5), (2,), 0, TOKENS)
    total_quantity = jax.random.uniform(jax.random.fold_in(sub_key, 6), (2, H), jnp.float32, 0.22, 0.45)
    match_count = (jnp.arange(TOKENS)[:, None] == spots[None, :]).astype(jnp.float32)
    sudden_spikes = jnp.dot(match_count, total_quantity)
    return (initial_gate - sudden_spikes).astype(jnp.bfloat16)


def levels(stream_key, extent, cuts, smallest, top_value):
    level = 1.0
    for axis_at, blocks in cuts:
        draws = jax.random.uniform(jax.random.fold_in(jax.random.fold_in(stream_key, 6), axis_at), (blocks,), jnp.float32, smallest / len(cuts), top_value / len(cuts))
        level = level * jnp.repeat(jnp.exp(draws), extent[axis_at] // blocks).reshape((-1,) + (1,) * (len(extent) - 1 - axis_at))
    return level


def scatter_about(rng, extent, deviation, most, split=(), kind=jnp.bfloat16):
    values = jax.random.normal(rng, extent, jnp.float32) * deviation
    if len(split) > 0:
        values = levels(rng, extent, split, -0.22, 0.18) * values
    return jnp.clip(values, min=-most, max=most).astype(kind)


def setup_inputs(seed: int = 0) -> dict:
    streams_of = jax.random.split(jax.random.key(seed), 8)
    queries = scatter_about(streams_of[0], (TOKENS, H * DK), 1.0, 6.0, ((0, 32),))
    key_rows = draw_key_rows(jax.random.fold_in(streams_of[7], 71), 0)
    value_rows = scatter_about(streams_of[2], (TOKENS, H * DV), 1.0, 6.0, ((0, 32),))
    beta_logit = draw_beta_logit(jax.random.fold_in(streams_of[7], 71), 0)
    log_gate = draw_log_gate(jax.random.fold_in(streams_of[7], 71), 0)
    out_grad = scatter_about(streams_of[5], (TOKENS, H * DV), 1.0, 6.0, ((0, 32),))
    block_states = scatter_about(streams_of[6], (N_OUTER, H, DK, DV), 0.5, 4.0, ((0, 4), (1, 8)), jnp.float32)
    return {"queries": queries, "key_rows": key_rows, "value_rows": value_rows, "beta_logit": beta_logit, "log_gate": log_gate, "out_grad": out_grad, "block_states": block_states}


precise = lax.Precision.HIGHEST

def unit_rows(matrix):
    return matrix * lax.rsqrt(lax.optimization_barrier(jnp.sum(matrix * matrix, axis=-1, keepdims=True)) + 1e-06)

def group_step(carried, inputs):
    state_now, transition = carried
    query_part, key_part, value_part, strength, gate_part = inputs
    group_len = query_part.shape[1]
    key_width = key_part.shape[2]
    row_index = jnp.arange(group_len)[:, None]
    col_index = jnp.arange(group_len)[None, :]
    inclusive = row_index >= col_index
    strictly_lower = row_index > col_index
    cumulative = jnp.cumsum(gate_part, axis=1)
    gaps = cumulative[:, :, None] - cumulative[:, None, :]
    decay_mat = jnp.where(inclusive, jnp.exp(jnp.where(inclusive, gaps, 0.0)), 0.0)
    key_gram = jnp.einsum('hid,hjd->hij', key_part, key_part, precision=precise)
    lower_mat = strength[:, :, None] * jnp.where(strictly_lower, decay_mat, 0.0) * key_gram
    unit_lower = lower_mat + jnp.eye(group_len, dtype=jnp.float32)
    growth = jnp.exp(cumulative)
    right_side = jnp.concatenate([(strength * growth)[:, :, None] * key_part, strength[:, :, None] * value_part], axis=2)
    solution_matrix = lax.linalg.triangular_solve(unit_lower, right_side, left_side=True, lower=True, unit_diagonal=True)
    write_keys = solution_matrix[:, :, :key_width]
    write_values = solution_matrix[:, :, key_width:]
    new_values = write_values - jnp.einsum('hcd,hde->hce', write_keys, state_now, precision=precise)
    scores = jnp.einsum('hid,hjd->hij', query_part, key_part, precision=precise) * decay_mat
    output = jnp.einsum('hcd,hde->hce', query_part * growth[:, :, None], state_now, precision=precise)
    output = output + jnp.einsum('hij,hje->hie', scores, new_values, precision=precise)
    tail_decay = jnp.exp(cumulative[:, -1:] - cumulative)
    tail_keys = key_part * tail_decay[:, :, None]
    last_growth = growth[:, -1][:, None, None]
    state_next = last_growth * state_now + jnp.einsum('hcd,hce->hde', tail_keys, new_values, precision=precise)
    step_trans = last_growth * jnp.eye(key_width, dtype=jnp.float32) - jnp.einsum('hcd,hce->hde', tail_keys, write_keys, precision=precise)
    transition = jnp.einsum('hij,hjk->hik', step_trans, transition, precision=precise)
    return ((state_next, transition), output)

def block_forward(queries, keys_in, values, logits, gates, start_state, group_size):
    head_count, length, key_width = queries.shape
    group_count = length // group_size

    def to_groups(array_in):
        shaped = array_in.reshape((head_count, group_count, group_size) + array_in.shape[2:])
        return jnp.moveaxis(shaped, 1, 0)
    inputs = (to_groups(unit_rows(queries)), to_groups(unit_rows(keys_in)), to_groups(values), to_groups(jax.nn.sigmoid(logits)), to_groups(gates))
    identity = jnp.broadcast_to(jnp.eye(key_width, dtype=jnp.float32), (head_count, key_width, key_width))
    (final_state, transition), outputs = lax.scan(group_step, (start_state, identity), inputs)
    outputs = jnp.moveaxis(outputs, 0, 1).reshape(head_count, length, -1)
    return (outputs, final_state, transition)

def reference(queries, key_rows, value_rows, beta_logit, log_gate, out_grad, block_states):
    per_block = TOKENS // N_OUTER

    def arrange(array_in, width):
        return array_in.astype(jnp.float32).reshape(N_OUTER, per_block, H, width).transpose(0, 2, 1, 3)

    def arrange_small(array_in):
        return array_in.astype(jnp.float32).reshape(N_OUTER, per_block, H).transpose(0, 2, 1)
    inputs = (arrange(queries, DK), arrange(key_rows, DK), arrange(value_rows, DV), arrange_small(beta_logit), arrange_small(log_gate), arrange(out_grad, DV), block_states)

    def backward(incoming, pieces):
        query_in, key_in, value_in, logit_in, gate_in, cotangent, start_state = pieces

        def forward(query_arg, key_arg, value_arg, logit_arg, gate_arg, state_arg):
            outputs, final_state, unused = block_forward(query_arg, key_arg, value_arg, logit_arg, gate_arg, state_arg, GROUP)
            return (outputs, final_state)
        unused_out, pull_back = jax.vjp(forward, query_in, key_in, value_in, logit_in, gate_in, start_state)
        gradients = pull_back((cotangent, incoming))
        return (gradients[5], gradients[:5])
    unused_carry, gradients = lax.scan(backward, jnp.zeros((H, DK, DV), jnp.float32), inputs, reverse=True)

    def restore(array_in):
        return array_in.transpose(0, 2, 1, 3).reshape(TOKENS, -1).astype(jnp.bfloat16)

    def restore_small(array_in):
        return array_in.transpose(0, 2, 1).reshape(TOKENS, H).astype(jnp.bfloat16)
    return (restore(gradients[0]), restore(gradients[1]), restore(gradients[2]), restore_small(gradients[3]), restore_small(gradients[4]))
```

```python
import functools

import jax
import jax.numpy as jnp
from jax import lax
from jax.experimental import pallas as pl
from jax.experimental.pallas import tpu as pltpu
from jax.sharding import PartitionSpec as P

D = 128
C = 128
BF = jnp.bfloat16
F32 = jnp.float32
DIMS = {"nn": ((1,), (0,)), "nt": ((1,), (1,)), "tn": ((0,), (0,))}


def split(x):
    hi = x.astype(BF)
    return hi, (x - hi.astype(F32)).astype(BF)


def exact(x):
    return x.astype(BF), None


def dot(a, b, mode):
    return lax.dot_general(a, b, (DIMS[mode], ((), ())), preferred_element_type=F32)


def mm(a, b, mode):
    ka = 0 if mode == "tn" else 1
    kb = 1 if mode == "nt" else 0
    (ah, al), (bh, bl) = a, b
    if al is None and bl is None:
        return dot(ah, bh, mode)
    if al is None:
        return dot(jnp.concatenate([ah, ah], ka), jnp.concatenate([bh, bl], kb), mode)
    left = jnp.concatenate([ah, al], ka)
    if bl is None:
        return dot(left, jnp.concatenate([bh, bh], kb), mode)
    top = jnp.concatenate([bh, bl], 1 - kb)
    low = jnp.concatenate([bh, jnp.zeros_like(bl)], 1 - kb)
    both = dot(left, jnp.concatenate([top, low], kb), mode)
    n = both.shape[1] // 2
    return both[:, :n] + both[:, n:]


def iotas():
    return lax.broadcasted_iota(jnp.int32, (C, C), 0), lax.broadcasted_iota(jnp.int32, (C, C), 1)


def ones_where(mask):
    return jnp.where(mask, 1.0, 0.0).astype(BF)


def unit(x):
    r = lax.rsqrt(jnp.sum(x * x, axis=1, keepdims=True) + 1e-06)
    return x * r, r


def decays(gate, row, col):
    wide = jnp.broadcast_to(gate, (C, C))
    rhs = jnp.concatenate([wide, jnp.where(row > col, wide, 0.0)], 1).astype(BF)
    both = dot(ones_where(row >= col), rhs, "nn")
    after = dot(ones_where(row < col), wide.astype(BF), "nn")
    pair = jnp.where(row >= col, jnp.exp(both[:, C:]), 0.0)
    return jnp.exp(both[:, :C]), jnp.exp(after), pair


def inverses(lowers, row, col):
    eye = jnp.where(row == col, 1.0, 0.0)
    done = [eye - jnp.where((row // 2 == col // 2), low, 0.0) for low in lowers]
    size = 2
    while size < C:
        pick = (row // (2 * size) == col // (2 * size)) & (row // size != col // size)
        halves = [split(t) for t in done]
        mids = [mm(t, split(jnp.where(pick, low, 0.0)), "nn") for t, low in zip(halves, lowers)]
        done = [t - mm(split(m), h, "nn") for t, m, h in zip(done, mids, halves)]
        size *= 2
    return done


def first_kernel(
    hpd, ng, step,
    q_ref, k_ref, v_ref, c_ref, b_ref, g_ref, s0_ref,
    turned_ref, start_ref, inv_ref, wk_ref, wv_ref, pr_ref, pc_ref, dec_ref, gram_ref,
    st_ref, base_ref, suf_ref,
    m_ref, mt_ref, add_ref, radd_ref,
):
    row, col = iotas()
    eye = row == col

    def body(i, carry):
        units = [(i * step + s, h) for s in range(step) for h in range(hpd)]
        data = []
        lowers = []
        for g, h in units:
            rows = pl.ds(pl.multiple_of(g * C, C), C)
            cols = slice(h * D, (h + 1) * D)
            beta = jax.nn.sigmoid(jnp.broadcast_to(b_ref[rows, h : h + 1], (C, C)))
            growth, tail, pair = decays(g_ref[rows, h : h + 1], row, col)
            qn, _ = unit(q_ref[rows, cols].astype(F32))
            kn, _ = unit(k_ref[rows, cols].astype(F32))
            qs, ks = split(qn), split(kn)
            left = (jnp.concatenate([qs[0], ks[0]], 0), jnp.concatenate([qs[1], ks[1]], 0))
            grams = mm(left, ks, "nt")
            scores = grams[:C] * pair
            gram = jnp.where(row > col, grams[C:] * pair, 0.0)
            u = g * hpd + h
            dec_ref[u] = pair
            gram_ref[u] = gram
            pr_ref[u] = scores
            lowers.append(beta * gram)
            cot = exact(c_ref[rows, cols])
            pc = mm(split(scores), cot, "tn")
            pc_ref[u] = pc
            qpart = mm(split(qn * growth), cot, "tn")
            data.append((u, kn, beta, growth, tail, v_ref[rows, cols].astype(F32), pc, qpart))
        for inv, (u, kn, beta, growth, tail, val, pc, qpart) in zip(inverses(lowers, row, col), data):
            inv_ref[u] = inv
            halves = split(inv)
            wk = mm(halves, split(beta * growth * kn), "nn")
            wv = mm(halves, split(beta * val), "nn")
            wk_ref[u] = wk
            wv_ref[u] = wv
            ws, ts = split(wk), split(kn * tail)
            last = jnp.where(eye, jnp.broadcast_to(growth[C - 1 :, :], (C, C)), 0.0)
            m_ref[u] = last - mm(ts, ws, "tn")
            mt_ref[u] = last - mm(ws, ts, "tn")
            add_ref[u] = mm(ts, split(wv), "tn")
            radd_ref[u] = qpart - mm(ws, split(pc), "tn")
        return carry

    lax.fori_loop(0, ng // step, body, 0)

    def chain(i, carry):
        out = []
        for h in range(hpd):
            state, grad, suffix = carry[h]
            u, w = i * hpd + h, (ng - 1 - i) * hpd + h
            st_ref[u] = state
            base_ref[w] = grad
            suf_ref[w] = suffix
            turned = split(mt_ref[w])
            out.append((
                mm(split(m_ref[u]), split(state), "nn") + add_ref[u],
                mm(turned, split(grad), "nn") + radd_ref[w],
                mm(turned, split(suffix), "nn"),
            ))
        return tuple(out)

    init = tuple(
        (s0_ref[h], jnp.zeros((D, D), F32), jnp.where(eye, 1.0, 0.0)) for h in range(hpd)
    )
    final = lax.fori_loop(0, ng, chain, init)
    for h in range(hpd):
        turned_ref[h] = final[h][2]
        start_ref[h] = final[h][1]


def second_kernel(
    hpd, ng, step, n_outer,
    pos_ref, turned_ref, start_ref, q_ref, k_ref, v_ref, c_ref, b_ref, g_ref,
    inv_ref, wk_ref, wv_ref, pr_ref, pc_ref, dec_ref, gram_ref, st_ref, base_ref, suf_ref,
    dq_ref, dk_ref, dv_ref, db_ref, dg_ref,
):
    row, col = iotas()
    position = pos_ref[0]

    def fold(i, carry):
        b = n_outer - 1 - i
        return tuple(
            jnp.where(
                b > position,
                mm(split(turned_ref[b, h]), split(carry[h]), "nn") + start_ref[b, h],
                carry[h],
            )
            for h in range(hpd)
        )

    incoming = lax.fori_loop(
        0, n_outer - 1, fold, tuple(jnp.zeros((D, D), F32) for _ in range(hpd))
    )
    arriving = [split(x) for x in incoming]
    upper = ones_where(row <= col)
    upper2 = jnp.concatenate([upper, upper], 1)
    lower = ones_where(row > col)
    lower2 = jnp.concatenate([lower, lower], 1)

    def body(i, carry):
        for s in range(step):
            for h in range(hpd):
                g = i * step + s
                u = g * hpd + h
                rows = pl.ds(pl.multiple_of(g * C, C), C)
                cols = slice(h * D, (h + 1) * D)
                beta = jax.nn.sigmoid(jnp.broadcast_to(b_ref[rows, h : h + 1], (C, C)))
                wide = jnp.broadcast_to(g_ref[rows, h : h + 1], (C, C)).astype(BF)
                growth = jnp.exp(dot(ones_where(row >= col), wide, "nn"))
                tail = jnp.exp(dot(ones_where(row < col), wide, "nn"))
                qn, qr = unit(q_ref[rows, cols].astype(F32))
                kn, kr = unit(k_ref[rows, cols].astype(F32))
                val = v_ref[rows, cols].astype(F32)
                cot = exact(c_ref[rows, cols])
                state = st_ref[u]
                ss = split(state)
                after = base_ref[u] + mm(split(suf_ref[u]), arriving[h], "nn")
                fs = split(after)
                tk = kn * tail
                dnew = pc_ref[u] + mm(split(tk), fs, "nn")
                new = wv_ref[u] - mm(split(wk_ref[u]), ss, "nn")
                ns = split(new)
                err = mm(split(inv_ref[u]), split(dnew), "tn")
                es = split(err)
                dkw = -mm(es, ss, "nt")
                dlow = jnp.where(row > col, -mm(es, ns, "nt"), 0.0)
                dsc = mm(cot, ns, "nt")
                dqg = mm(cot, ss, "nt")
                dtk = mm(ns, fs, "nt")
                pair = dec_ref[u]
                gram = gram_ref[u]
                b1 = split(dsc * pair)
                b2 = split(dlow * beta * pair)
                qs, ks = split(qn), split(kn)
                b12 = (jnp.concatenate([b1[0], b2[0]], 0), jnp.concatenate([b1[1], b2[1]], 0))
                fwd = mm(b12, ks, "nn")
                dqn = fwd[:C] + growth * dqg
                dkn = (
                    fwd[C:] + mm(b1, qs, "tn") + mm(b2, ks, "tn")
                    + beta * growth * dkw + tail * dtk
                )
                dq_ref[rows, cols] = (
                    qr * (dqn - qn * jnp.sum(dqn * qn, axis=1, keepdims=True))
                ).astype(BF)
                dk_ref[rows, cols] = (
                    kr * (dkn - kn * jnp.sum(dkn * kn, axis=1, keepdims=True))
                ).astype(BF)
                dv_ref[rows, cols] = (beta * err).astype(BF)
                kgrow = kn * growth * dkw
                dlg = dlow * gram
                dbeta = jnp.sum(dlg + kgrow + err * val, axis=1, keepdims=True)
                b0 = beta[:, :1]
                db_ref[rows, h : h + 1] = dbeta * b0 * (1.0 - b0)
                z = dsc * pr_ref[u] + beta * dlg
                x = dqg * qn * growth + beta * kgrow
                y = dtk * tk
                zx = split(jnp.concatenate([z, x], 1))
                up = dot(upper2, jnp.concatenate(zx, 0), "nn")
                down = dot(lower2, jnp.concatenate(split(y), 0), "nn")
                total = jnp.sum(
                    jnp.sum(state * after * growth[C - 1 :, :], axis=1, keepdims=True),
                    axis=0, keepdims=True,
                )
                dg_ref[rows, h : h + 1] = (
                    jnp.sum(
                        jnp.where(row > col, up[:, :C], 0.0) + up[:, C:] + down,
                        axis=1, keepdims=True,
                    )
                    + total
                )
        return carry

    lax.fori_loop(0, ng // step, body, 0)


VM = pl.BlockSpec(memory_space=pltpu.VMEM)


def run_first(q, k, v, cot, logit, gate, s0, interpret=False):
    hpd, ng = q.shape[1] // D, q.shape[0] // C
    step = max(1, 4 // hpd)
    big = jax.ShapeDtypeStruct((hpd * ng, D, D), F32)
    small = jax.ShapeDtypeStruct((hpd, D, D), F32)
    return pl.pallas_call(
        functools.partial(first_kernel, hpd, ng, step),
        out_shape=(small, small) + (big,) * 10,
        in_specs=[VM] * 7,
        out_specs=(VM,) * 12,
        scratch_shapes=[pltpu.VMEM((hpd * ng, D, D), F32)] * 4,
        compiler_params=pltpu.CompilerParams(vmem_limit_bytes=56 << 20),
        interpret=interpret,
    )(q, k, v, cot, logit, gate, s0)


def run_second(pos, turned, start, q, k, v, cot, logit, gate, rest, interpret=False):
    hpd, ng = q.shape[1] // D, q.shape[0] // C
    step = max(1, 2 // hpd)
    big = jax.ShapeDtypeStruct(q.shape, BF)
    thin = jax.ShapeDtypeStruct((q.shape[0], hpd), F32)
    return pl.pallas_call(
        functools.partial(second_kernel, hpd, ng, step, turned.shape[0]),
        out_shape=(big, big, big, thin, thin),
        in_specs=[pl.BlockSpec(memory_space=pltpu.SMEM)] + [VM] * 18,
        out_specs=(VM,) * 5,
        compiler_params=pltpu.CompilerParams(vmem_limit_bytes=56 << 20),
        interpret=interpret,
    )(pos, turned, start, q, k, v, cot, logit, gate, *rest)


def shards(queries, key_rows, value_rows, beta_logit, log_gate, out_grad, block_states):
    def inward(x):
        return lax.all_to_all(x, "inner", split_axis=1, concat_axis=0, tiled=True)

    def outward(x):
        return lax.all_to_all(x, "inner", split_axis=0, concat_axis=1, tiled=True)

    q, k, v, cot = (inward(x) for x in (queries, key_rows, value_rows, out_grad))
    logit = inward(beta_logit).astype(F32)
    gate = inward(log_gate).astype(F32)
    first = run_first(q, k, v, cot, logit, gate, block_states[0])
    turned = lax.all_gather(first[0], "outer", axis=0)
    start = lax.all_gather(first[1], "outer", axis=0)
    pos = lax.axis_index("outer").astype(jnp.int32).reshape(1)
    out = run_second(pos, turned, start, q, k, v, cot, logit, gate, first[2:])
    return (
        outward(out[0]), outward(out[1]), outward(out[2]),
        outward(out[3].astype(BF)), outward(out[4].astype(BF)),
    )


def solution(mesh):
    wide = P(("outer", "inner"), None)
    return jax.shard_map(
        shards,
        mesh=mesh,
        in_specs=(wide,) * 6 + (P("outer", "inner", None, None),),
        out_specs=(wide,) * 5,
        check_vma=False,
    )
```

```python
import functools

import jax
import jax.numpy as jnp
from jax import lax
from jax.experimental import pallas as pl
from jax.experimental.pallas import tpu as pltpu
from jax.sharding import PartitionSpec as P

D = 128
C = 128
BF = jnp.bfloat16
F32 = jnp.float32
MESH = pl.DeviceIdType.MESH
VM = pl.BlockSpec(memory_space=pltpu.VMEM)
DIMS = {"nn": ((1,), (0,)), "nt": ((1,), (1,)), "tn": ((0,), (0,))}


def split(x):
    hi = x.astype(BF)
    return hi, (x - hi.astype(F32)).astype(BF)


def exact(x):
    return x.astype(BF), None


def dot(a, b, mode):
    return lax.dot_general(a, b, (DIMS[mode], ((), ())), preferred_element_type=F32)


def mm(a, b, mode):
    ka = 0 if mode == "tn" else 1
    kb = 1 if mode == "nt" else 0
    (ah, al), (bh, bl) = a, b
    if al is None and bl is None:
        return dot(ah, bh, mode)
    if al is None:
        return dot(jnp.concatenate([ah, ah], ka), jnp.concatenate([bh, bl], kb), mode)
    left = jnp.concatenate([ah, al], ka)
    if bl is None:
        return dot(left, jnp.concatenate([bh, bh], kb), mode)
    top = jnp.concatenate([bh, bl], 1 - kb)
    low = jnp.concatenate([bh, jnp.zeros_like(bl)], 1 - kb)
    both = dot(left, jnp.concatenate([top, low], kb), mode)
    n = both.shape[1] // 2
    return both[:, :n] + both[:, n:]


def iotas():
    return lax.broadcasted_iota(jnp.int32, (C, C), 0), lax.broadcasted_iota(jnp.int32, (C, C), 1)


def ones_where(mask):
    return jnp.where(mask, 1.0, 0.0).astype(BF)


def unit(x):
    r = lax.rsqrt(jnp.sum(x * x, axis=1, keepdims=True) + 1e-06)
    return x * r, r


def decays(gate, row, col):
    wide = gate
    rhs = jnp.concatenate([wide, jnp.where(row > col, wide, 0.0)], 1).astype(BF)
    both = dot(ones_where(row >= col), rhs, "nn")
    after = dot(ones_where(row < col), wide.astype(BF), "nn")
    pair = jnp.where(row >= col, jnp.exp(both[:, C:]), 0.0)
    return jnp.exp(both[:, :C]), jnp.exp(after), pair


def inverses(lowers, row, col):
    eye = jnp.where(row == col, 1.0, 0.0)
    done = [eye - jnp.where((row // 2 == col // 2), low, 0.0) for low in lowers]
    size = 2
    while size < C:
        pick = (row // (2 * size) == col // (2 * size)) & (row // size != col // size)
        halves = [split(t) for t in done]
        mids = [mm(t, split(jnp.where(pick, low, 0.0)), "nn") for t, low in zip(halves, lowers)]
        done = [t - mm(split(m), h, "nn") for t, m, h in zip(done, mids, halves)]
        size *= 2
    return done


def head_columns(b_ref, g_ref, h):
    heads = b_ref.shape[1]
    pick = ones_where(lax.broadcasted_iota(jnp.int32, (heads, C), 0) == h)
    return jax.nn.sigmoid(dot(b_ref[...], pick, "nn")), dot(g_ref[...], pick, "nn")


def grams(qn, kn, pair, row, col):
    qs, ks = split(qn), split(kn)
    left = (jnp.concatenate([qs[0], ks[0]], 0), jnp.concatenate([qs[1], ks[1]], 0))
    both = mm(left, ks, "nt")
    return both[:C] * pair, jnp.where(row > col, both[C:] * pair, 0.0)


def first_kernel(
    count, b_ref, g_ref, q_ref, k_ref, v_ref, c_ref,
    m_ref, mt_ref, add_ref, radd_ref, inv_ref, wk_ref, wv_ref, pc_ref,
):
    row, col = iotas()
    eye = row == col
    data, lowers = [], []
    for s in range(count):
        cols = slice(s * D, (s + 1) * D)
        beta, gate = head_columns(b_ref, g_ref, pl.program_id(0) * count + s)
        growth, tail, pair = decays(gate, row, col)
        qn, _ = unit(q_ref[:, cols].astype(F32))
        kn, _ = unit(k_ref[:, cols].astype(F32))
        scores, gram = grams(qn, kn, pair, row, col)
        lowers.append(beta * gram)
        cot = exact(c_ref[:, cols])
        pc = mm(split(scores), cot, "tn")
        pc_ref[s] = pc
        qpart = mm(split(qn * growth), cot, "tn")
        data.append((kn, beta, growth, tail, v_ref[:, cols].astype(F32), pc, qpart))
    for s, inv in enumerate(inverses(lowers, row, col)):
        kn, beta, growth, tail, val, pc, qpart = data[s]
        inv_ref[s] = inv
        halves = split(inv)
        wk = mm(halves, split(beta * growth * kn), "nn")
        wv = mm(halves, split(beta * val), "nn")
        wk_ref[s] = wk
        wv_ref[s] = wv
        ws, ts = split(wk), split(kn * tail)
        last = jnp.where(eye, jnp.broadcast_to(growth[C - 1 :, :], (C, C)), 0.0)
        m_ref[s] = last - mm(ts, ws, "tn")
        mt_ref[s] = last - mm(ws, ts, "tn")
        add_ref[s] = mm(ts, split(wv), "tn")
        radd_ref[s] = qpart - mm(ws, split(pc), "tn")


def chain_kernel(
    heads, n, n_outer,
    s0_ref, m_ref, mt_ref, add_ref, radd_ref,
    st_ref, after_ref,
    sout, bin_ref, bout, oin, oout,
    s0send, fsend, frecv, bsend, brecv, osend, orecv, rsend,
):
    o, i = lax.axis_index("outer"), lax.axis_index("inner")
    hpd = s0_ref.shape[0]
    barrier = pltpu.get_barrier_semaphore()
    for d in range(1, n):
        pl.semaphore_signal(
            barrier, inc=1, device_id=(o, lax.rem(i + d, n)), device_id_type=MESH
        )
    for d in range(1, n_outer):
        pl.semaphore_signal(
            barrier, inc=1, device_id=(lax.rem(o + d, n_outer), i), device_id_type=MESH
        )
    pl.semaphore_wait(barrier, n + n_outer - 2)

    def remote(src, dst, send, recv, target):
        return pltpu.make_async_remote_copy(
            src_ref=src, dst_ref=dst, send_sem=send, recv_sem=recv,
            device_id=target, device_id_type=MESH,
        )

    def start_copy(j):
        h = i * hpd + j
        return remote(s0_ref.at[j], st_ref.at[h], s0send.at[j], frecv.at[h], (o, 0))

    def up_copy(h):
        return remote(sout.at[h], st_ref.at[h], fsend.at[h], frecv.at[h], (o, lax.rem(i + 1, n)))

    def down_copy(h):
        return remote(
            bout.at[h], bin_ref.at[h], bsend.at[h], brecv.at[h], (o, lax.rem(i + n - 1, n))
        )

    def outer_copy(h):
        return remote(
            oout.at[h], oin.at[h], osend.at[h], orecv.at[h],
            (lax.rem(o + n_outer - 1, n_outer), i),
        )

    def relay_copy(h, hop):
        return remote(
            oin.at[h], oin.at[h], rsend.at[h, hop - 1], orecv.at[h], (o, lax.rem(i + hop, n))
        )

    even = lax.rem(i, 2) == 0
    relays = o < n_outer - 1
    near = relays & even & (i + 1 < n)
    far = relays & even & (i + 2 < n)

    @pl.when(i == 0)
    def _():
        for j in range(hpd):
            pltpu.make_async_copy(s0_ref.at[j], st_ref.at[j], frecv.at[j]).start()

    @pl.when(i > 0)
    def _():
        for j in range(hpd):
            start_copy(j).start()

    lag_up = 2 * i
    lag_down = 2 * (n - 1 - i)
    lag_outer = 2 * (n - 1) + 2 * (n_outer - 1 - o)
    lag_in = lag_outer + 2 * (i // 2 + lax.rem(i, 2))

    def tick(t, carry):
        up = t - lag_up

        @pl.when((up >= 0) & (up < heads))
        def _():
            pltpu.make_async_copy(st_ref.at[up], st_ref.at[up], frecv.at[up]).wait()

            @pl.when(i < n - 1)
            def _():
                sout[up] = mm(split(m_ref[up]), split(st_ref[up]), "nn") + add_ref[up]
                up_copy(up).start()

        down = t - lag_down

        @pl.when((down >= 0) & (down < heads))
        def _():
            @pl.when(i == n - 1)
            def _():
                row, col = iotas()
                bin_ref[down, :, :D] = jnp.zeros((D, D), F32)
                bin_ref[down, :, D:] = jnp.where(row == col, 1.0, 0.0)
                bout[down, :, :D] = radd_ref[down]
                bout[down, :, D:] = mt_ref[down]

            @pl.when(i < n - 1)
            def _():
                down_copy(down).wait_recv()
                turned = split(mt_ref[down])
                bout[down, :, :D] = (
                    mm(turned, split(bin_ref[down, :, :D]), "nn") + radd_ref[down]
                )
                bout[down, :, D:] = mm(turned, split(bin_ref[down, :, D:]), "nn")

            @pl.when(i > 0)
            def _():
                down_copy(down).start()

        last = t - lag_in

        @pl.when((last >= 0) & (last < heads))
        def _():
            @pl.when(relays)
            def _():
                outer_copy(last).wait_recv()

            @pl.when(near)
            def _():
                relay_copy(last, 1).start()

            @pl.when(far)
            def _():
                relay_copy(last, 2).start()

            @pl.when((i == 0) & (o > 0) & relays)
            def _():
                oout[last] = (
                    mm(split(bout[last, :, D:]), split(oin[last]), "nn") + bout[last, :, :D]
                )

            @pl.when((i == 0) & (o > 0) & (o == n_outer - 1))
            def _():
                oout[last] = bout[last, :, :D]

            @pl.when((i == 0) & (o > 0))
            def _():
                outer_copy(last).start()

            @pl.when(relays)
            def _():
                after_ref[last] = bin_ref[last, :, :D] + mm(
                    split(bin_ref[last, :, D:]), split(oin[last]), "nn"
                )

            @pl.when(o == n_outer - 1)
            def _():
                after_ref[last] = bin_ref[last, :, :D]

        return carry

    ticks = heads + 2 * (n - 1) + 2 * (n_outer - 1) + 2 * ((n - 1) // 2 + (n - 1) % 2)
    lax.fori_loop(0, ticks, tick, 0)

    @pl.when(i > 0)
    def _():
        for j in range(hpd):
            start_copy(j).wait_send()

    def finish(h, carry):
        @pl.when(i < n - 1)
        def _():
            up_copy(h).wait_send()

        @pl.when(i > 0)
        def _():
            down_copy(h).wait_send()

        @pl.when((i == 0) & (o > 0))
        def _():
            outer_copy(h).wait_send()

        @pl.when(near)
        def _():
            relay_copy(h, 1).wait_send()

        @pl.when(far)
        def _():
            relay_copy(h, 2).wait_send()

        return carry

    lax.fori_loop(0, heads, finish, 0)


def final_kernel(
    count, b_ref, g_ref, q_ref, k_ref, v_ref, c_ref,
    inv_ref, wk_ref, wv_ref, pc_ref, st_ref, after_ref,
    dq_ref, dk_ref, dv_ref, db_ref, dg_ref, db_acc, dg_acc,
):
    row, col = iotas()
    step = pl.program_id(0)

    @pl.when(step == 0)
    def _():
        db_acc[...] = jnp.zeros_like(db_acc)
        dg_acc[...] = jnp.zeros_like(dg_acc)

    upper = ones_where(row <= col)
    upper2 = jnp.concatenate([upper, upper], 1)
    lower = ones_where(row > col)
    lower2 = jnp.concatenate([lower, lower], 1)
    lane = lax.broadcasted_iota(jnp.int32, db_acc.shape, 1)
    for s in range(count):
        cols = slice(s * D, (s + 1) * D)
        h = step * count + s
        beta, gate = head_columns(b_ref, g_ref, h)
        growth, tail, pair = decays(gate, row, col)
        qn, qr = unit(q_ref[:, cols].astype(F32))
        kn, kr = unit(k_ref[:, cols].astype(F32))
        scores, gram = grams(qn, kn, pair, row, col)
        val = v_ref[:, cols].astype(F32)
        cot = exact(c_ref[:, cols])
        state, after = st_ref[s], after_ref[s]
        ss, fs = split(state), split(after)
        tk = kn * tail
        new = wv_ref[s] - mm(split(wk_ref[s]), ss, "nn")
        ns = split(new)
        dsc = mm(cot, ns, "nt")
        dqg = mm(cot, ss, "nt")
        dnew = pc_ref[s] + mm(split(tk), fs, "nn")
        err = mm(split(inv_ref[s]), split(dnew), "tn")
        es = split(err)
        dkw = -mm(es, ss, "nt")
        dlow = jnp.where(row > col, -mm(es, ns, "nt"), 0.0)
        dtk = mm(ns, fs, "nt")
        b1 = split(dsc * pair)
        b2 = split(dlow * beta * pair)
        qs, ks = split(qn), split(kn)
        b12 = (jnp.concatenate([b1[0], b2[0]], 0), jnp.concatenate([b1[1], b2[1]], 0))
        fwd = mm(b12, ks, "nn")
        dqn = fwd[:C] + growth * dqg
        dkn = (
            fwd[C:] + mm(b1, qs, "tn") + mm(b2, ks, "tn") + beta * growth * dkw + tail * dtk
        )
        dq_ref[:, cols] = (qr * (dqn - qn * jnp.sum(dqn * qn, axis=1, keepdims=True))).astype(BF)
        dk_ref[:, cols] = (kr * (dkn - kn * jnp.sum(dkn * kn, axis=1, keepdims=True))).astype(BF)
        dv_ref[:, cols] = (beta * err).astype(BF)
        kgrow = kn * growth * dkw
        dlg = dlow * gram
        dbeta = jnp.sum((dlg + kgrow + err * val) * (beta * (1.0 - beta)), axis=1, keepdims=True)
        z = dsc * scores + beta * dlg
        x = dqg * qn * growth + beta * kgrow
        zx = split(jnp.concatenate([z, x], 1))
        up = dot(upper2, jnp.concatenate(zx, 0), "nn")
        below = dot(lower2, jnp.concatenate(split(dtk * tk), 0), "nn")
        total = jnp.sum(
            jnp.sum(state * after * growth[C - 1 :, :], axis=1, keepdims=True),
            axis=0, keepdims=True,
        )
        dgate = total + jnp.sum(
            jnp.where(row > col, up[:, :C], 0.0) + up[:, C:] + below, axis=1, keepdims=True
        )
        db_acc[...] = jnp.where(lane == h, dbeta, db_acc[...])
        dg_acc[...] = jnp.where(lane == h, dgate, dg_acc[...])

    @pl.when(step == pl.num_programs(0) - 1)
    def _():
        db_ref[...] = db_acc[...].astype(BF)
        dg_ref[...] = dg_acc[...].astype(BF)


def head_specs(count, heads):
    small = pl.BlockSpec((C, heads), lambda j: (0, 0))
    token = pl.BlockSpec((C, count * D), lambda j: (0, j))
    matrix = pl.BlockSpec((count, D, D), lambda j: (j, 0, 0))
    return small, token, matrix


PARAMS = pltpu.CompilerParams(vmem_limit_bytes=56 << 20)


def run_first(logit, gate, q, k, v, cot, count=4, interpret=False):
    heads = logit.shape[1]
    small, token, matrix = head_specs(count, heads)
    big = jax.ShapeDtypeStruct((heads, D, D), F32)
    return pl.pallas_call(
        functools.partial(first_kernel, count),
        grid=(heads // count,),
        out_shape=(big,) * 8,
        in_specs=[small] * 2 + [token] * 4,
        out_specs=(matrix,) * 8,
        compiler_params=PARAMS,
        interpret=interpret,
    )(logit, gate, q, k, v, cot)


def run_chain(s0, m, mt, add, radd, n, n_outer):
    heads = m.shape[0]
    big = jax.ShapeDtypeStruct((heads, D, D), F32)
    one = pltpu.VMEM((heads, D, D), F32)
    two = pltpu.VMEM((heads, D, 2 * D), F32)
    sems = pltpu.SemaphoreType.DMA((heads,))
    return pl.pallas_call(
        functools.partial(chain_kernel, heads, n, n_outer),
        out_shape=(big, big),
        in_specs=[VM] * 5,
        out_specs=(VM, VM),
        scratch_shapes=[
            one, two, two, one, one,
            pltpu.SemaphoreType.DMA((s0.shape[0],)), sems, sems, sems, sems, sems, sems,
            pltpu.SemaphoreType.DMA((heads, 2)),
        ],
        compiler_params=pltpu.CompilerParams(
            vmem_limit_bytes=56 << 20, collective_id=0, has_side_effects=True
        ),
    )(s0, m, mt, add, radd)


def run_final(logit, gate, q, k, v, cot, rest, count=2, interpret=False):
    heads = logit.shape[1]
    small, token, matrix = head_specs(count, heads)
    big = jax.ShapeDtypeStruct(q.shape, BF)
    thin = jax.ShapeDtypeStruct(logit.shape, BF)
    return pl.pallas_call(
        functools.partial(final_kernel, count),
        grid=(heads // count,),
        out_shape=(big, big, big, thin, thin),
        in_specs=[small] * 2 + [token] * 4 + [matrix] * 6,
        out_specs=(token, token, token, small, small),
        scratch_shapes=[pltpu.VMEM((C, heads), F32)] * 2,
        compiler_params=PARAMS,
        interpret=interpret,
    )(logit, gate, q, k, v, cot, *rest)


def shards(n, n_outer, queries, key_rows, value_rows, beta_logit, log_gate, out_grad, block_states):
    tokens = (beta_logit, log_gate, queries, key_rows, value_rows, out_grad)
    m, mt, add, radd, inv, wk, wv, pc = run_first(*tokens)
    state, after = run_chain(block_states[0], m, mt, add, radd, n, n_outer)
    return run_final(*tokens, (inv, wk, wv, pc, state, after))


def solution(mesh):
    wide = P(("outer", "inner"), None)
    return jax.shard_map(
        functools.partial(shards, mesh.shape["inner"], mesh.shape["outer"]),
        mesh=mesh,
        in_specs=(wide,) * 6 + (P("outer", "inner", None, None),),
        out_specs=(wide,) * 5,
        check_vma=False,
    )
```

```python
import functools

import jax
import jax.numpy as jnp
from jax import lax
from jax.experimental import pallas as pl
from jax.experimental.pallas import tpu as pltpu
from jax.sharding import PartitionSpec as P

D = 128
C = 128
BF = jnp.bfloat16
F32 = jnp.float32
MESH = pl.DeviceIdType.MESH
VM = pl.BlockSpec(memory_space=pltpu.VMEM)
DIMS = {"nn": ((1,), (0,)), "nt": ((1,), (1,)), "tn": ((0,), (0,))}


def split(x):
    hi = x.astype(BF)
    return hi, (x - hi.astype(F32)).astype(BF)


def exact(x):
    return x.astype(BF), None


def dot(a, b, mode):
    return lax.dot_general(a, b, (DIMS[mode], ((), ())), preferred_element_type=F32)


def mm(a, b, mode):
    ka = 0 if mode == "tn" else 1
    kb = 1 if mode == "nt" else 0
    (ah, al), (bh, bl) = a, b
    if al is None and bl is None:
        return dot(ah, bh, mode)
    if al is None:
        return dot(jnp.concatenate([ah, ah], ka), jnp.concatenate([bh, bl], kb), mode)
    left = jnp.concatenate([ah, al], ka)
    if bl is None:
        return dot(left, jnp.concatenate([bh, bh], kb), mode)
    top = jnp.concatenate([bh, bl], 1 - kb)
    low = jnp.concatenate([bh, jnp.zeros_like(bl)], 1 - kb)
    both = dot(left, jnp.concatenate([top, low], kb), mode)
    n = both.shape[1] // 2
    return both[:, :n] + both[:, n:]


def iotas():
    return lax.broadcasted_iota(jnp.int32, (C, C), 0), lax.broadcasted_iota(jnp.int32, (C, C), 1)


def ones_where(mask):
    return jnp.where(mask, 1.0, 0.0).astype(BF)


def unit(x):
    r = lax.rsqrt(jnp.sum(x * x, axis=1, keepdims=True) + 1e-06)
    return x * r, r


def decays(gate, row, col):
    wide = gate
    rhs = jnp.concatenate([wide, jnp.where(row > col, wide, 0.0)], 1).astype(BF)
    both = dot(ones_where(row >= col), rhs, "nn")
    after = dot(ones_where(row < col), wide.astype(BF), "nn")
    pair = jnp.where(row >= col, jnp.exp(both[:, C:]), 0.0)
    return jnp.exp(both[:, :C]), jnp.exp(after), pair


def inverses(lowers, row, col):
    eye = jnp.where(row == col, 1.0, 0.0)
    done = [eye - jnp.where((row // 2 == col // 2), low, 0.0) for low in lowers]
    size = 2
    while size < C:
        pick = (row // (2 * size) == col // (2 * size)) & (row // size != col // size)
        halves = [split(t) for t in done]
        mids = [mm(t, split(jnp.where(pick, low, 0.0)), "nn") for t, low in zip(halves, lowers)]
        done = [t - mm(split(m), h, "nn") for t, m, h in zip(done, mids, halves)]
        size *= 2
    return done


def head_columns(b_ref, g_ref, h):
    heads = b_ref.shape[1]
    pick = ones_where(lax.broadcasted_iota(jnp.int32, (heads, C), 0) == h)
    return jax.nn.sigmoid(dot(b_ref[...], pick, "nn")), dot(g_ref[...], pick, "nn")


def grams(qn, kn, pair, row, col):
    qs, ks = split(qn), split(kn)
    left = (jnp.concatenate([qs[0], ks[0]], 0), jnp.concatenate([qs[1], ks[1]], 0))
    both = mm(left, ks, "nt")
    return both[:C] * pair, jnp.where(row > col, both[C:] * pair, 0.0)


def columns(h):
    return pl.ds(pl.multiple_of(h * D, D), D)


def group_stage(hs, args, keep):
    b_ref, g_ref, q_ref, k_ref, v_ref, c_ref = args
    row, col = iotas()
    eye = row == col
    data, lowers = [], []
    for h in hs:
        beta, gate = head_columns(b_ref, g_ref, h)
        growth, tail, pair = decays(gate, row, col)
        qn, _ = unit(q_ref[:, columns(h)].astype(F32))
        kn, _ = unit(k_ref[:, columns(h)].astype(F32))
        scores, gram = grams(qn, kn, pair, row, col)
        lowers.append(beta * gram)
        for name, value in (
            ("beta", beta), ("growth", growth), ("tail", tail),
            ("pair", pair), ("scores", scores), ("gram", gram),
        ):
            keep[name][h] = value
        cot = exact(c_ref[:, columns(h)])
        pc = mm(split(scores), cot, "tn")
        keep["pc"][h] = pc
        qpart = mm(split(qn * growth), cot, "tn")
        data.append((kn, beta, growth, tail, v_ref[:, columns(h)].astype(F32), pc, qpart))
    for h, inv, rest in zip(hs, inverses(lowers, row, col), data):
        kn, beta, growth, tail, val, pc, qpart = rest
        keep["inv"][h] = inv
        halves = split(inv)
        wk = mm(halves, split(beta * growth * kn), "nn")
        wv = mm(halves, split(beta * val), "nn")
        keep["wk"][h] = wk
        keep["wv"][h] = wv
        ws, ts = split(wk), split(kn * tail)
        last = jnp.where(eye, jnp.broadcast_to(growth[C - 1 :, :], (C, C)), 0.0)
        keep["m"][h] = last - mm(ts, ws, "tn")
        keep["mt"][h] = last - mm(ws, ts, "tn")
        keep["add"][h] = mm(ts, split(wv), "tn")
        keep["radd"][h] = qpart - mm(ws, split(pc), "tn")


def state_stage(hs, args, keep, dq_ref):
    _, _, q_ref, k_ref, _, c_ref = args
    for h in hs:
        qn, qr = unit(q_ref[:, columns(h)].astype(F32))
        kn, _ = unit(k_ref[:, columns(h)].astype(F32))
        cot = exact(c_ref[:, columns(h)])
        ss = split(keep["st"][h])
        new = keep["wv"][h] - mm(split(keep["wk"][h]), ss, "nn")
        ns = split(new)
        dsc = mm(cot, ns, "nt")
        dqg = keep["growth"][h] * mm(cot, ss, "nt")
        b1 = split(dsc * keep["pair"][h])
        dqn = mm(b1, split(kn), "nn") + dqg
        dq_ref[:, columns(h)] = (
            qr * (dqn - qn * jnp.sum(dqn * qn, axis=1, keepdims=True))
        ).astype(BF)
        keep["wv"][h] = new
        keep["wk"][h] = mm(b1, split(qn), "tn")
        keep["z"][h] = dsc * keep["scores"][h]
        keep["x"][h] = dqg * qn


def grad_stage(hs, args, keep, dk_ref, dv_ref, db_acc, dg_acc):
    _, _, _, k_ref, v_ref, _ = args
    row, col = iotas()
    upper = ones_where(row <= col)
    upper2 = jnp.concatenate([upper, upper], 1)
    lower = ones_where(row > col)
    lower2 = jnp.concatenate([lower, lower], 1)
    lane = lax.broadcasted_iota(jnp.int32, db_acc.shape, 1)
    for h in hs:
        kn, kr = unit(k_ref[:, columns(h)].astype(F32))
        val = v_ref[:, columns(h)].astype(F32)
        beta, growth, tail = keep["beta"][h], keep["growth"][h], keep["tail"][h]
        state = keep["st"][h]
        after = keep["bin"][h, :, :D] + mm(
            split(keep["bin"][h, :, D:]), split(keep["oin"][h]), "nn"
        )
        ss, fs, ns, ks = split(state), split(after), split(keep["wv"][h]), split(kn)
        tk = kn * tail
        dnew = keep["pc"][h] + mm(split(tk), fs, "nn")
        dtk = mm(ns, fs, "nt")
        err = mm(split(keep["inv"][h]), split(dnew), "tn")
        es = split(err)
        dkw = -mm(es, ss, "nt")
        dlow = jnp.where(row > col, -mm(es, ns, "nt"), 0.0)
        b2 = split(dlow * beta * keep["pair"][h])
        kgrow = growth * dkw
        dkn = (
            keep["wk"][h] + mm(b2, ks, "nn") + mm(b2, ks, "tn") + beta * kgrow + tail * dtk
        )
        dk_ref[:, columns(h)] = (
            kr * (dkn - kn * jnp.sum(dkn * kn, axis=1, keepdims=True))
        ).astype(BF)
        dv_ref[:, columns(h)] = (beta * err).astype(BF)
        kgrow = kn * kgrow
        dlg = dlow * keep["gram"][h]
        dbeta = jnp.sum((dlg + kgrow + err * val) * (beta * (1.0 - beta)), axis=1, keepdims=True)
        z = keep["z"][h] + beta * dlg
        x = keep["x"][h] + beta * kgrow
        zx = split(jnp.concatenate([z, x], 1))
        up = dot(upper2, jnp.concatenate(zx, 0), "nn")
        below = dot(lower2, jnp.concatenate(split(dtk * tk), 0), "nn")
        total = jnp.sum(
            jnp.sum(state * after * growth[C - 1 :, :], axis=1, keepdims=True),
            axis=0, keepdims=True,
        )
        dgate = total + jnp.sum(
            jnp.where(row > col, up[:, :C], 0.0) + up[:, C:] + below, axis=1, keepdims=True
        )
        db_acc[...] = jnp.where(lane == h, dbeta, db_acc[...])
        dg_acc[...] = jnp.where(lane == h, dgate, dg_acc[...])


KEPT = (
    "m", "mt", "add", "radd", "inv", "wk", "wv", "pc", "beta", "growth", "tail",
    "pair", "scores", "gram", "z", "x", "st", "sout", "oin", "oout",
)
QUAD, DUO = 4, 2


def chain_kernel(
    heads, n, n_outer,
    b_ref, g_ref, q_ref, k_ref, v_ref, c_ref, s0_ref,
    dq_ref, dk_ref, dv_ref, db_ref, dg_ref,
    *scratch,
):
    args = (b_ref, g_ref, q_ref, k_ref, v_ref, c_ref)
    keep = dict(zip(KEPT, scratch))
    bin_ref, bout, db_acc, dg_acc = scratch[len(KEPT) : len(KEPT) + 4]
    s0send, fsend, frecv, bsend, brecv, osend, orecv, rsend = scratch[len(KEPT) + 4 :]
    keep["bin"] = bin_ref
    m_ref, mt_ref, add_ref, radd_ref = (keep[x] for x in ("m", "mt", "add", "radd"))
    st_ref, sout, oin, oout = (keep[x] for x in ("st", "sout", "oin", "oout"))
    o, i = lax.axis_index("outer"), lax.axis_index("inner")
    hpd = s0_ref.shape[0]
    barrier = pltpu.get_barrier_semaphore()
    for d in range(1, n):
        pl.semaphore_signal(
            barrier, inc=1, device_id=(o, lax.rem(i + d, n)), device_id_type=MESH
        )
    for d in range(1, n_outer):
        pl.semaphore_signal(
            barrier, inc=1, device_id=(lax.rem(o + d, n_outer), i), device_id_type=MESH
        )
    pl.semaphore_wait(barrier, n + n_outer - 2)

    def remote(src, dst, send, recv, target):
        return pltpu.make_async_remote_copy(
            src_ref=src, dst_ref=dst, send_sem=send, recv_sem=recv,
            device_id=target, device_id_type=MESH,
        )

    def start_copy(j):
        h = i * hpd + j
        return remote(s0_ref.at[j], st_ref.at[h], s0send.at[j], frecv.at[h], (o, 0))

    def up_copy(h):
        return remote(sout.at[h], st_ref.at[h], fsend.at[h], frecv.at[h], (o, lax.rem(i + 1, n)))

    def down_copy(h):
        return remote(
            bout.at[h], bin_ref.at[h], bsend.at[h], brecv.at[h], (o, lax.rem(i + n - 1, n))
        )

    def outer_copy(h):
        return remote(
            oout.at[h], oin.at[h], osend.at[h], orecv.at[h],
            (lax.rem(o + n_outer - 1, n_outer), i),
        )

    def relay_copy(h, hop):
        return remote(
            oin.at[h], oin.at[h], rsend.at[h, hop - 1], orecv.at[h], (o, lax.rem(i + hop, n))
        )

    even = lax.rem(i, 2) == 0
    relays = o < n_outer - 1
    near = relays & even & (i + 1 < n)
    far = relays & even & (i + 2 < n)

    @pl.when(i == 0)
    def _():
        for j in range(hpd):
            pltpu.make_async_copy(s0_ref.at[j], st_ref.at[j], frecv.at[j]).start()

    @pl.when(i > 0)
    def _():
        for j in range(hpd):
            start_copy(j).start()

    lag_up = 2 * i
    lag_down = 2 * (n - 1 - i)
    lag_outer = 2 * (n - 1) + 2 * (n_outer - 1 - o)
    lag_in = lag_outer + 2 * (i // 2 + lax.rem(i, 2))
    lag_state = jnp.maximum(heads, lag_up + DUO - 1)
    lag_grad = jnp.maximum(lag_in + DUO - 1, lag_state + 1)
    db_acc[...] = jnp.zeros_like(db_acc)
    dg_acc[...] = jnp.zeros_like(dg_acc)

    @pl.when(o == n_outer - 1)
    def _():
        oin[...] = jnp.zeros_like(oin)

    def tick(t, carry):
        @pl.when((lax.rem(t, QUAD) == 0) & (t < heads))
        def _():
            group_stage([t + s for s in range(QUAD)], args, keep)

        up = t - lag_up

        @pl.when((up >= 0) & (up < heads))
        def _():
            pltpu.make_async_copy(st_ref.at[up], st_ref.at[up], frecv.at[up]).wait()

            @pl.when(i < n - 1)
            def _():
                sout[up] = mm(split(m_ref[up]), split(st_ref[up]), "nn") + add_ref[up]
                up_copy(up).start()

        down = t - lag_down

        @pl.when((down >= 0) & (down < heads))
        def _():
            @pl.when(i == n - 1)
            def _():
                row, col = iotas()
                bin_ref[down, :, :D] = jnp.zeros((D, D), F32)
                bin_ref[down, :, D:] = jnp.where(row == col, 1.0, 0.0)
                bout[down, :, :D] = radd_ref[down]
                bout[down, :, D:] = mt_ref[down]

            @pl.when(i < n - 1)
            def _():
                down_copy(down).wait_recv()
                turned = split(mt_ref[down])
                bout[down, :, :D] = (
                    mm(turned, split(bin_ref[down, :, :D]), "nn") + radd_ref[down]
                )
                bout[down, :, D:] = mm(turned, split(bin_ref[down, :, D:]), "nn")

            @pl.when(i > 0)
            def _():
                down_copy(down).start()

        last = t - lag_in

        @pl.when((last >= 0) & (last < heads))
        def _():
            @pl.when(relays)
            def _():
                outer_copy(last).wait_recv()

            @pl.when(near)
            def _():
                relay_copy(last, 1).start()

            @pl.when(far)
            def _():
                relay_copy(last, 2).start()

            @pl.when((i == 0) & (o > 0) & relays)
            def _():
                oout[last] = (
                    mm(split(bout[last, :, D:]), split(oin[last]), "nn") + bout[last, :, :D]
                )

            @pl.when((i == 0) & (o > 0) & (o == n_outer - 1))
            def _():
                oout[last] = bout[last, :, :D]

            @pl.when((i == 0) & (o > 0))
            def _():
                outer_copy(last).start()

        first = t - lag_state

        @pl.when((first >= 0) & (first < heads) & (lax.rem(first, DUO) == 0))
        def _():
            state_stage([first + s for s in range(DUO)], args, keep, dq_ref)

        done = t - lag_grad

        @pl.when((done >= 0) & (done < heads) & (lax.rem(done, DUO) == 0))
        def _():
            grad_stage([done + s for s in range(DUO)], args, keep, dk_ref, dv_ref, db_acc, dg_acc)

        return carry

    lax.fori_loop(0, lag_grad + heads, tick, 0)
    db_ref[...] = db_acc[...].astype(BF)
    dg_ref[...] = dg_acc[...].astype(BF)

    @pl.when(i > 0)
    def _():
        for j in range(hpd):
            start_copy(j).wait_send()

    def finish(h, carry):
        @pl.when(i < n - 1)
        def _():
            up_copy(h).wait_send()

        @pl.when(i > 0)
        def _():
            down_copy(h).wait_send()

        @pl.when((i == 0) & (o > 0))
        def _():
            outer_copy(h).wait_send()

        @pl.when(near)
        def _():
            relay_copy(h, 1).wait_send()

        @pl.when(far)
        def _():
            relay_copy(h, 2).wait_send()

        return carry

    lax.fori_loop(0, heads, finish, 0)


def shards(n, n_outer, queries, key_rows, value_rows, beta_logit, log_gate, out_grad, block_states):
    heads = beta_logit.shape[1]
    big = jax.ShapeDtypeStruct(queries.shape, BF)
    thin = jax.ShapeDtypeStruct(beta_logit.shape, BF)
    one = pltpu.VMEM((heads, D, D), F32)
    two = pltpu.VMEM((heads, D, 2 * D), F32)
    acc = pltpu.VMEM((C, heads), F32)
    sems = pltpu.SemaphoreType.DMA((heads,))
    return pl.pallas_call(
        functools.partial(chain_kernel, heads, n, n_outer),
        out_shape=(big, big, big, thin, thin),
        in_specs=[VM] * 7,
        out_specs=(VM,) * 5,
        scratch_shapes=[one] * len(KEPT) + [two, two, acc, acc] + [
            pltpu.SemaphoreType.DMA((block_states.shape[1],)), sems, sems, sems, sems, sems, sems,
            pltpu.SemaphoreType.DMA((heads, 2)),
        ],
        compiler_params=pltpu.CompilerParams(
            vmem_limit_bytes=56 << 20, collective_id=0, has_side_effects=True
        ),
    )(beta_logit, log_gate, queries, key_rows, value_rows, out_grad, block_states[0])


def solution(mesh):
    wide = P(("outer", "inner"), None)
    return jax.shard_map(
        functools.partial(shards, mesh.shape["inner"], mesh.shape["outer"]),
        mesh=mesh,
        in_specs=(wide,) * 6 + (P("outer", "inner", None, None),),
        out_specs=(wide,) * 5,
        check_vma=False,
    )
```

```python
import functools

import jax
import jax.numpy as jnp
from jax import lax
from jax.experimental import pallas as pl
from jax.experimental.pallas import tpu as pltpu
from jax.sharding import PartitionSpec as P

D = 128
C = 128
BF = jnp.bfloat16
F32 = jnp.float32
MESH = pl.DeviceIdType.MESH
VM = pl.BlockSpec(memory_space=pltpu.VMEM)
DIMS = {"nn": ((1,), (0,)), "nt": ((1,), (1,)), "tn": ((0,), (0,))}


def split(x):
    hi = x.astype(BF)
    return hi, (x - hi.astype(F32)).astype(BF)


def exact(x):
    return x.astype(BF), None


def dot(a, b, mode):
    return lax.dot_general(a, b, (DIMS[mode], ((), ())), preferred_element_type=F32)


def mm(a, b, mode):
    ka = 0 if mode == "tn" else 1
    kb = 1 if mode == "nt" else 0
    (ah, al), (bh, bl) = a, b
    if al is None and bl is None:
        return dot(ah, bh, mode)
    if al is None:
        return dot(jnp.concatenate([ah, ah], ka), jnp.concatenate([bh, bl], kb), mode)
    left = jnp.concatenate([ah, al], ka)
    if bl is None:
        return dot(left, jnp.concatenate([bh, bh], kb), mode)
    top = jnp.concatenate([bh, bl], 1 - kb)
    low = jnp.concatenate([bh, jnp.zeros_like(bl)], 1 - kb)
    both = dot(left, jnp.concatenate([top, low], kb), mode)
    n = both.shape[1] // 2
    return both[:, :n] + both[:, n:]


def iotas():
    return lax.broadcasted_iota(jnp.int32, (C, C), 0), lax.broadcasted_iota(jnp.int32, (C, C), 1)


def ones_where(mask):
    return jnp.where(mask, 1.0, 0.0).astype(BF)


def unit(x):
    r = lax.rsqrt(jnp.sum(x * x, axis=1, keepdims=True) + 1e-06)
    return x * r, r


def decays(gate, row, col):
    wide = gate
    rhs = jnp.concatenate([wide, jnp.where(row > col, wide, 0.0)], 1).astype(BF)
    both = dot(ones_where(row >= col), rhs, "nn")
    after = dot(ones_where(row < col), wide.astype(BF), "nn")
    pair = jnp.where(row >= col, jnp.exp(both[:, C:]), 0.0)
    return jnp.exp(both[:, :C]), jnp.exp(after), pair


def inverses(lowers, row, col):
    eye = jnp.where(row == col, 1.0, 0.0)
    done = [eye - jnp.where((row // 2 == col // 2), low, 0.0) for low in lowers]
    size = 2
    while size < C:
        pick = (row // (2 * size) == col // (2 * size)) & (row // size != col // size)
        halves = [split(t) for t in done]
        mids = [mm(t, split(jnp.where(pick, low, 0.0)), "nn") for t, low in zip(halves, lowers)]
        done = [t - mm(split(m), h, "nn") for t, m, h in zip(done, mids, halves)]
        size *= 2
    return done


def head_columns(b_ref, g_ref, h):
    heads = b_ref.shape[0]
    pick = ones_where(lax.broadcasted_iota(jnp.int32, (heads, C), 0) == h)
    return jax.nn.sigmoid(dot(b_ref[...], pick, "tn")), dot(g_ref[...], pick, "tn")


def grams(qn, kn, pair, row, col):
    qs, ks = split(qn), split(kn)
    left = (jnp.concatenate([qs[0], ks[0]], 0), jnp.concatenate([qs[1], ks[1]], 0))
    both = mm(left, ks, "nt")
    return both[:C] * pair, jnp.where(row > col, both[C:] * pair, 0.0)


def columns(h):
    return pl.ds(pl.multiple_of(h * D, D), D)


def group_stage(hs, args, keep):
    b_ref, g_ref, q_ref, k_ref, v_ref, c_ref = args
    row, col = iotas()
    eye = row == col
    data, lowers = [], []
    for h in hs:
        beta, gate = head_columns(b_ref, g_ref, h)
        growth, tail, pair = decays(gate, row, col)
        qn, _ = unit(q_ref[:, columns(h)].astype(F32))
        kn, _ = unit(k_ref[:, columns(h)].astype(F32))
        scores, gram = grams(qn, kn, pair, row, col)
        lowers.append(beta * gram)
        for name, value in (
            ("beta", beta), ("growth", growth), ("tail", tail),
            ("pair", pair), ("scores", scores), ("gram", gram),
        ):
            keep[name][h] = value
        cot = exact(c_ref[:, columns(h)])
        pc = mm(split(scores), cot, "tn")
        keep["pc"][h] = pc
        qpart = mm(split(qn * growth), cot, "tn")
        data.append((kn, beta, growth, tail, v_ref[:, columns(h)].astype(F32), pc, qpart))
    for h, inv, rest in zip(hs, inverses(lowers, row, col), data):
        kn, beta, growth, tail, val, pc, qpart = rest
        keep["inv"][h] = inv
        halves = split(inv)
        wk = mm(halves, split(beta * growth * kn), "nn")
        wv = mm(halves, split(beta * val), "nn")
        keep["wk"][h] = wk
        keep["wv"][h] = wv
        ws, ts = split(wk), split(kn * tail)
        last = jnp.where(eye, jnp.broadcast_to(growth[C - 1 :, :], (C, C)), 0.0)
        keep["m"][h] = jnp.concatenate(split(last - mm(ts, ws, "tn")), 1)
        keep["mt"][h] = jnp.concatenate(split(last - mm(ws, ts, "tn")), 1)
        keep["add"][h] = mm(ts, split(wv), "tn")
        keep["radd"][h] = qpart - mm(ws, split(pc), "tn")


def state_stage(hs, args, keep, dq_ref):
    _, _, q_ref, k_ref, _, c_ref = args
    for h in hs:
        qn, qr = unit(q_ref[:, columns(h)].astype(F32))
        kn, _ = unit(k_ref[:, columns(h)].astype(F32))
        cot = exact(c_ref[:, columns(h)])
        ss = split(keep["st"][h])
        new = keep["wv"][h] - mm(split(keep["wk"][h]), ss, "nn")
        ns = split(new)
        dsc = mm(cot, ns, "nt")
        dqg = keep["growth"][h] * mm(cot, ss, "nt")
        b1 = split(dsc * keep["pair"][h])
        dqn = mm(b1, split(kn), "nn") + dqg
        dq_ref[:, columns(h)] = (
            qr * (dqn - qn * jnp.sum(dqn * qn, axis=1, keepdims=True))
        ).astype(BF)
        keep["wv"][h] = new
        keep["wk"][h] = mm(b1, split(qn), "tn")
        keep["z"][h] = dsc * keep["scores"][h]
        keep["x"][h] = dqg * qn


def grad_stage(hs, args, keep, dk_ref, dv_ref, db_acc, dg_acc):
    _, _, _, k_ref, v_ref, _ = args
    row, col = iotas()
    upper = ones_where(row <= col)
    upper2 = jnp.concatenate([upper, upper], 1)
    lower = ones_where(row > col)
    lower2 = jnp.concatenate([lower, lower], 1)
    lane = lax.broadcasted_iota(jnp.int32, db_acc.shape, 1)
    for h in hs:
        kn, kr = unit(k_ref[:, columns(h)].astype(F32))
        val = v_ref[:, columns(h)].astype(F32)
        beta, growth, tail = keep["beta"][h], keep["growth"][h], keep["tail"][h]
        state = keep["st"][h]
        after = keep["bin"][h, :, :D] + mm(
            split(keep["bin"][h, :, D:]), split(keep["oin"][h]), "nn"
        )
        ss, fs, ns, ks = split(state), split(after), split(keep["wv"][h]), split(kn)
        tk = kn * tail
        dnew = keep["pc"][h] + mm(split(tk), fs, "nn")
        dtk = mm(ns, fs, "nt")
        err = mm(split(keep["inv"][h]), split(dnew), "tn")
        es = split(err)
        dkw = -mm(es, ss, "nt")
        dlow = jnp.where(row > col, -mm(es, ns, "nt"), 0.0)
        b2 = split(dlow * beta * keep["pair"][h])
        kgrow = growth * dkw
        dkn = (
            keep["wk"][h] + mm(b2, ks, "nn") + mm(b2, ks, "tn") + beta * kgrow + tail * dtk
        )
        dk_ref[:, columns(h)] = (
            kr * (dkn - kn * jnp.sum(dkn * kn, axis=1, keepdims=True))
        ).astype(BF)
        dv_ref[:, columns(h)] = (beta * err).astype(BF)
        kgrow = kn * kgrow
        dlg = dlow * keep["gram"][h]
        dbeta = jnp.sum((dlg + kgrow + err * val) * (beta * (1.0 - beta)), axis=1, keepdims=True)
        z = keep["z"][h] + beta * dlg
        x = keep["x"][h] + beta * kgrow
        zx = split(jnp.concatenate([z, x], 1))
        up = dot(upper2, jnp.concatenate(zx, 0), "nn")
        below = dot(lower2, jnp.concatenate(split(dtk * tk), 0), "nn")
        total = jnp.sum(
            jnp.sum(state * after * growth[C - 1 :, :], axis=1, keepdims=True),
            axis=0, keepdims=True,
        )
        dgate = total + jnp.sum(
            jnp.where(row > col, up[:, :C], 0.0) + up[:, C:] + below, axis=1, keepdims=True
        )
        db_acc[...] = jnp.where(lane == h, dbeta, db_acc[...])
        dg_acc[...] = jnp.where(lane == h, dgate, dg_acc[...])


KEPT = (
    "add", "radd", "inv", "wk", "wv", "pc", "beta", "growth", "tail",
    "pair", "scores", "gram", "z", "x", "st", "sout", "oin", "oout",
)
QUAD, DUO = 4, 2


def pair_of(ref, h):
    return ref[h, :, :D], ref[h, :, D:]


def chain_kernel(
    heads, n, n_outer,
    b_ref, g_ref, q_ref, k_ref, v_ref, c_ref, s0_ref,
    dq_ref, dk_ref, dv_ref, db_ref, dg_ref,
    *scratch,
):
    args = (b_ref, g_ref, q_ref, k_ref, v_ref, c_ref)
    keep = dict(zip(KEPT, scratch))
    bin_ref, bout, m_ref, mt_ref, db_acc, dg_acc = scratch[len(KEPT) : len(KEPT) + 6]
    s0send, fsend, frecv, bsend, brecv, osend, orecv, rsend = scratch[len(KEPT) + 6 :]
    keep["bin"], keep["m"], keep["mt"] = bin_ref, m_ref, mt_ref
    add_ref, radd_ref = keep["add"], keep["radd"]
    st_ref, sout, oin, oout = (keep[x] for x in ("st", "sout", "oin", "oout"))
    o, i = lax.axis_index("outer"), lax.axis_index("inner")
    hpd = s0_ref.shape[0]
    barrier = pltpu.get_barrier_semaphore()
    for d in range(1, n):
        pl.semaphore_signal(
            barrier, inc=1, device_id=(o, lax.rem(i + d, n)), device_id_type=MESH
        )
    for d in range(1, n_outer):
        pl.semaphore_signal(
            barrier, inc=1, device_id=(lax.rem(o + d, n_outer), i), device_id_type=MESH
        )
    pl.semaphore_wait(barrier, n + n_outer - 2)

    def remote(src, dst, send, recv, target):
        return pltpu.make_async_remote_copy(
            src_ref=src, dst_ref=dst, send_sem=send, recv_sem=recv,
            device_id=target, device_id_type=MESH,
        )

    def start_copy(j):
        h = i * hpd + j
        return remote(s0_ref.at[j], st_ref.at[h], s0send.at[j], frecv.at[h], (o, 0))

    def up_copy(h):
        return remote(sout.at[h], st_ref.at[h], fsend.at[h], frecv.at[h], (o, lax.rem(i + 1, n)))

    def down_copy(h):
        return remote(
            bout.at[h], bin_ref.at[h], bsend.at[h], brecv.at[h], (o, lax.rem(i + n - 1, n))
        )

    def outer_copy(h):
        return remote(
            oout.at[h], oin.at[h], osend.at[h], orecv.at[h],
            (lax.rem(o + n_outer - 1, n_outer), i),
        )

    def relay_copy(h, hop):
        return remote(
            oin.at[h], oin.at[h], rsend.at[h, hop - 1], orecv.at[h], (o, lax.rem(i + hop, n))
        )

    even = lax.rem(i, 2) == 0
    relays = o < n_outer - 1
    near = relays & even & (i + 1 < n)
    far = relays & even & (i + 2 < n)

    @pl.when(i == 0)
    def _():
        for j in range(hpd):
            pltpu.make_async_copy(s0_ref.at[j], st_ref.at[j], frecv.at[j]).start()

    @pl.when(i > 0)
    def _():
        for j in range(hpd):
            start_copy(j).start()

    lag_up = 2 * i
    lag_down = 2 * (n - 1 - i)
    lag_outer = 2 * (n - 1) + 2 * (n_outer - 1 - o)
    lag_in = lag_outer + 2 * (i // 2 + lax.rem(i, 2))
    lag_state = jnp.maximum(heads, lag_up + DUO - 1)
    lag_grad = jnp.maximum(lag_in + DUO - 1, lag_state + 1)
    db_acc[...] = jnp.zeros_like(db_acc)
    dg_acc[...] = jnp.zeros_like(dg_acc)

    @pl.when(o == n_outer - 1)
    def _():
        oin[...] = jnp.zeros_like(oin)

    @pl.when(i == n - 1)
    def _():
        row, col = iotas()
        ident = jnp.where(row == col, 1.0, 0.0)
        for h in range(heads):
            bin_ref[h] = jnp.concatenate([jnp.zeros_like(ident), ident], 1)

    def tick(t, carry):
        @pl.when((lax.rem(t, QUAD) == 0) & (t < heads))
        def _():
            group_stage([t + s for s in range(QUAD)], args, keep)

        up, down = t - lag_up, t - lag_down
        up_ok = (up >= 0) & (up < heads)
        down_ok = (down >= 0) & (down < heads)

        @pl.when(up_ok)
        def _():
            pltpu.make_async_copy(st_ref.at[up], st_ref.at[up], frecv.at[up]).wait()

        @pl.when(down_ok & (i < n - 1))
        def _():
            down_copy(down).wait_recv()

        @pl.when(up_ok | down_ok)
        def _():
            at_up, at_down = jnp.where(up_ok, up, heads), jnp.where(down_ok, down, heads)
            moved = mm(pair_of(m_ref, at_up), split(st_ref[at_up]), "nn") + add_ref[at_up]
            back = mm(pair_of(mt_ref, at_down), split(bin_ref[at_down]), "nn")
            grad = back[:, :D] + radd_ref[at_down]
            sout[at_up] = moved
            bout[at_down] = jnp.concatenate([grad, back[:, D:]], 1)

        @pl.when(up_ok & (i < n - 1))
        def _():
            up_copy(up).start()

        @pl.when(down_ok & (i > 0))
        def _():
            down_copy(down).start()

        last = t - lag_in

        @pl.when((last >= 0) & (last < heads))
        def _():
            @pl.when(relays)
            def _():
                outer_copy(last).wait_recv()

            @pl.when(near)
            def _():
                relay_copy(last, 1).start()

            @pl.when(far)
            def _():
                relay_copy(last, 2).start()

            @pl.when((i == 0) & (o > 0))
            def _():
                oout[last] = (
                    mm(split(bout[last, :, D:]), split(oin[last]), "nn") + bout[last, :, :D]
                )

            @pl.when((i == 0) & (o > 0))
            def _():
                outer_copy(last).start()

        first = t - lag_state

        @pl.when((first >= 0) & (first < heads) & (lax.rem(first, DUO) == 0))
        def _():
            state_stage([first + s for s in range(DUO)], args, keep, dq_ref)

        done = t - lag_grad

        @pl.when((done >= 0) & (done < heads) & (lax.rem(done, DUO) == 0))
        def _():
            grad_stage([done + s for s in range(DUO)], args, keep, dk_ref, dv_ref, db_acc, dg_acc)

        return carry

    lax.fori_loop(0, lag_grad + heads, tick, 0)
    db_ref[...] = db_acc[...].T[:heads].astype(BF)
    dg_ref[...] = dg_acc[...].T[:heads].astype(BF)

    @pl.when(i > 0)
    def _():
        for j in range(hpd):
            start_copy(j).wait_send()

    def finish(h, carry):
        @pl.when(i < n - 1)
        def _():
            up_copy(h).wait_send()

        @pl.when(i > 0)
        def _():
            down_copy(h).wait_send()

        @pl.when((i == 0) & (o > 0))
        def _():
            outer_copy(h).wait_send()

        @pl.when(near)
        def _():
            relay_copy(h, 1).wait_send()

        @pl.when(far)
        def _():
            relay_copy(h, 2).wait_send()

        return carry

    lax.fori_loop(0, heads, finish, 0)


def shards(n, n_outer, queries, key_rows, value_rows, beta_logit, log_gate, out_grad, block_states):
    heads = beta_logit.shape[1]
    big = jax.ShapeDtypeStruct(queries.shape, BF)
    thin = jax.ShapeDtypeStruct((heads, C), BF)
    one = pltpu.VMEM((heads + 1, D, D), F32)
    two = pltpu.VMEM((heads + 1, D, 2 * D), F32)
    halves = pltpu.VMEM((heads + 1, D, 2 * D), BF)
    acc = pltpu.VMEM((C, D), F32)
    sems = pltpu.SemaphoreType.DMA((heads,))
    dq, dk, dv, db, dg = pl.pallas_call(
        functools.partial(chain_kernel, heads, n, n_outer),
        out_shape=(big, big, big, thin, thin),
        in_specs=[VM] * 7,
        out_specs=(VM,) * 5,
        scratch_shapes=[one] * len(KEPT) + [two, two, halves, halves, acc, acc] + [
            pltpu.SemaphoreType.DMA((block_states.shape[1],)), sems, sems, sems, sems, sems, sems,
            pltpu.SemaphoreType.DMA((heads, 2)),
        ],
        compiler_params=pltpu.CompilerParams(
            vmem_limit_bytes=56 << 20, collective_id=0, has_side_effects=True
        ),
    )(beta_logit.T, log_gate.T, queries, key_rows, value_rows, out_grad, block_states[0])
    return dq, dk, dv, db.T, dg.T


def solution(mesh):
    wide = P(("outer", "inner"), None)
    return jax.shard_map(
        functools.partial(shards, mesh.shape["inner"], mesh.shape["outer"]),
        mesh=mesh,
        in_specs=(wide,) * 6 + (P("outer", "inner", None, None),),
        out_specs=(wide,) * 5,
        check_vma=False,
    )
```
